32 devices in a mesh: groups: 2 (over x), seq: 16 (over z, y, core).
Axes of the slice: x: 2, y: 2, z: 4, core: 2. Of those that a mesh axis runs over, the one named last changes fastest.
Arguments:
- clip_tokens: bfloat16 [32, 128, 512], P(('groups', 'seq')), parts along dimension 0, may hold values from -6 to 6
- spatial_qkv: bfloat16 [512, 1536], replicated, may hold values from -4.6403883 to 4.6403883
- spatial_out: bfloat16 [512, 512], replicated, may hold values from -0.5 to 0.5
- temporal_qkv: bfloat16 [512, 1536], replicated, may hold values from -4.6403883 to 4.6403883
- temporal_out: bfloat16 [512, 512], replicated, may hold values from -0.5 to 0.5
- mlp_up: bfloat16 [512, 2048], replicated, may hold values from -0.25 to 0.25
- mlp_down: bfloat16 [2048, 512], replicated, may hold values from -0.25 to 0.25
Outputs:
- layer_out: bfloat16 [32, 128, 512], P(('groups', 'seq')), parts along dimension 0
The draws below stay inside these ranges and needn't reach their ends.
There are 2 independent parts, one for each index of `groups`. The reference program is written for one: setup_inputs(seed, part) draws one part's arguments, and reference() takes and returns one part's arrays. A program takes and returns all parts, laid end to end along the dimension named above; an argument that names none is the same for every part. Nothing has to cross between parts.
All inputs are finite; a program needn't handle non-finite values.
Results may differ from the reference program's by a relative error of at most 0.013.
Values may be sent and summed in bfloat16 or wider, within the bound.
A program may use at most 128 MiB of HBM per device.

```python
import jax
import jax.numpy as jnp
from jax import lax

D = 512
HEADS = 8
HEAD_DIM = 64
FF = 2048
PATCH_DEV = 8
FRAMES = 16
PATCHES = 128


def projection_draw(key):
    scale = D ** (-0.5)
    matrix_draw = jnp.clip(jax.random.normal(key, (D, 3 * D), jnp.float32), -5.0, 5.0) * scale
    return matrix_draw.astype(jnp.bfloat16)


def draw_spatial_qkv(key, part):
    return projection_draw(jax.random.fold_in(key, 101))


def draw_temporal_qkv(key, part):
    return projection_draw(jax.random.fold_in(key, 202))


def shard_levels(rng, dims, shards, smallest, top_value):
    def one(axis_at, shards_of):
        steps = jax.random.uniform(jax.random.fold_in(jax.random.fold_in(rng, 6), axis_at), (shards_of,), jnp.float32, smallest / len(shards), top_value / len(shards))
        return jnp.repeat(jnp.exp(steps), dims[axis_at] // shards_of).reshape((-1,) + (1,) * (len(dims) - axis_at - 1))

    gain = one(*shards[0])
    for cut in shards[1:]:
        gain = gain * one(*cut)
    return gain


def gaussian(key, extent, deviation, reach, split=(), held_as=jnp.bfloat16):
    drawn = jax.random.normal(key, extent, jnp.float32) * deviation
    if len(split) > 0:
        drawn = shard_levels(key, extent, split, -0.22, 0.18) * drawn
    return jnp.clip(drawn, min=-reach, max=reach).astype(held_as)


def setup_inputs(seed: int = 0, part: int = 0) -> dict:
    streams_of = jax.random.split(jax.random.key(seed), 8)
    own_keys = jax.random.split(jax.random.fold_in(streams_of[7], part), 8)
    clip_tokens = gaussian(own_keys[0], (FRAMES, PATCHES, D), 1.0, 6.0, ((0, 16),))
    spatial_qkv = draw_spatial_qkv(jax.random.fold_in(streams_of[7], 71), part)
    spatial_out = gaussian(streams_of[2], (D, D), (D // 4) ** -0.5, 0.5)
    temporal_qkv = draw_temporal_qkv(jax.random.fold_in(streams_of[7], 71), part)
    temporal_out = gaussian(streams_of[4], (D, D), (D // 4) ** -0.5, 0.5)
    mlp_up = gaussian(streams_of[5], (D, FF), D ** -0.5, 0.25)
    mlp_down = gaussian(streams_of[6], (FF, D), (FF // 4) ** -0.5, 0.25)
    return {"clip_tokens": clip_tokens, "spatial_qkv": spatial_qkv, "spatial_out": spatial_out, "temporal_qkv": temporal_qkv, "temporal_out": temporal_out, "mlp_up": mlp_up, "mlp_down": mlp_down}


def norm_rows(values):
    center = values - lax.optimization_barrier(jnp.mean(values, axis=-1, keepdims=True))
    spread = lax.optimization_barrier(jnp.mean(center * center, axis=-1, keepdims=True))
    return (center * lax.rsqrt(spread + 1e-05)).astype(jnp.bfloat16)

def softmax_rows(scores):
    row_max = lax.optimization_barrier(jnp.max(scores, axis=-1, keepdims=True))
    raised = jnp.exp(scores - row_max)
    return (raised / lax.optimization_barrier(jnp.sum(raised, axis=-1, keepdims=True))).astype(jnp.bfloat16)

def spatial_frame(frame_rows, w_qkv, w_out):
    packed = jnp.dot(norm_rows(frame_rows.astype(jnp.float32)), w_qkv, preferred_element_type=jnp.float32)
    packed = packed.astype(jnp.bfloat16).reshape(PATCHES, 3, HEADS, HEAD_DIM).astype(jnp.float32)
    scores = jnp.einsum('qhd,khd->hqk', packed[:, 0], packed[:, 1]) * HEAD_DIM ** (-0.5)
    weights = softmax_rows(scores).astype(jnp.float32)
    attended = jnp.einsum('hqk,khd->qhd', weights, packed[:, 2]).astype(jnp.bfloat16).reshape(PATCHES, D)
    merged = frame_rows.astype(jnp.float32) + jnp.dot(attended, w_out, preferred_element_type=jnp.float32)
    return merged.astype(jnp.bfloat16)

def temporal_block(tokens, w_qkv, w_out):
    frames, count_rows, model_width = tokens.shape
    flat_rows = tokens.reshape(frames * count_rows, model_width)
    packed = jnp.dot(norm_rows(flat_rows.astype(jnp.float32)), w_qkv, preferred_element_type=jnp.float32)
    packed = packed.astype(jnp.bfloat16).reshape(frames, count_rows, 3, HEADS, HEAD_DIM).astype(jnp.float32)
    scores = jnp.einsum('fkhd,gkhd->khfg', packed[:, :, 0], packed[:, :, 1]) * HEAD_DIM ** (-0.5)
    weights = softmax_rows(scores).astype(jnp.float32)
    attended = jnp.einsum('khfg,gkhd->fkhd', weights, packed[:, :, 2]).astype(jnp.bfloat16)
    attended = attended.reshape(frames * count_rows, model_width)
    merged = flat_rows.astype(jnp.float32) + jnp.dot(attended, w_out, preferred_element_type=jnp.float32)
    return merged.astype(jnp.bfloat16)

def feed_forward(tokens, w_up, w_down):
    raised = jnp.dot(norm_rows(tokens.astype(jnp.float32)), w_up, preferred_element_type=jnp.float32)
    hidden = jax.nn.gelu(raised, approximate=True).astype(jnp.bfloat16)
    merged = tokens.astype(jnp.float32) + jnp.dot(hidden, w_down, preferred_element_type=jnp.float32)
    return merged.astype(jnp.bfloat16)

def reference(clip_tokens, spatial_qkv, spatial_out, temporal_qkv, temporal_out, mlp_up, mlp_down):
    mixed = lax.map(lambda frame_rows: spatial_frame(frame_rows, spatial_qkv, spatial_out), clip_tokens)
    blocks = mixed.reshape(FRAMES, PATCHES // PATCH_DEV, PATCH_DEV, D).transpose(1, 0, 2, 3)

    def one_block(tokens):
        after_time = temporal_block(tokens, temporal_qkv, temporal_out)
        return feed_forward(after_time, mlp_up, mlp_down).reshape(FRAMES, PATCH_DEV, D)
    finished = lax.map(one_block, blocks)
    return finished.transpose(1, 0, 2, 3).reshape(FRAMES, PATCHES, D)
```

```python
import functools
import math

import jax
import jax.numpy as jnp
from jax import lax
from jax.experimental import pallas as pl
from jax.experimental.pallas import tpu as pltpu
from jax.sharding import PartitionSpec as P

HEADS = 8
LANES = 128
MESH = pl.DeviceIdType.MESH
F32 = jnp.float32
BF16 = jnp.bfloat16


def norm_rows(values):
    center = values - jnp.mean(values, axis=-1, keepdims=True)
    spread = jnp.mean(center * center, axis=-1, keepdims=True)
    return (center * lax.rsqrt(spread + 1e-05)).astype(BF16)


def gelu(u):
    return 0.5 * u * (1.0 + jnp.tanh(math.sqrt(2.0 / math.pi) * (u + 0.044715 * (u * u * u))))


def dot(a, b):
    return jnp.dot(a, b, preferred_element_type=F32)


def blocks_of(count, body):
    if count <= 2:
        for i in range(count):
            body(i)
    else:
        def step(i, carry):
            body(i)
            return carry

        lax.fori_loop(0, count, step, 0)


def attend(packed, first_row, rows, width, head_width, same_slot):
    total = packed.shape[0]
    per_block = LANES // head_width
    lane = lax.broadcasted_iota(jnp.int32, (rows, LANES), 1)
    ones = jnp.ones((total, LANES), BF16)
    scale = head_width ** (-0.5) * math.log2(math.e)
    if same_slot:
        query_at = lax.broadcasted_iota(jnp.int32, (per_block * rows, total), 0)
        key_at = lax.broadcasted_iota(jnp.int32, (per_block * rows, total), 1)
        allowed = lax.rem(query_at, same_slot) == lax.rem(key_at, same_slot)
    outs = []
    for block in range(width // LANES):
        q = packed[pl.ds(first_row, rows), pl.ds(block * LANES, LANES)]
        k = packed[:, pl.ds(width + block * LANES, LANES)]
        v = packed[:, pl.ds(2 * width + block * LANES, LANES)]
        split = [
            jnp.where((lane >= h * head_width) & (lane < (h + 1) * head_width), q, jnp.zeros_like(q))
            for h in range(per_block)
        ]
        scores = lax.dot_general(
            jnp.concatenate(split, axis=0), k, (((1,), (1,)), ((), ())), preferred_element_type=F32
        )
        if same_slot:
            scores = jnp.where(allowed, scores, -1e30)
        top = jnp.max(scores, axis=-1, keepdims=True)
        raised = jnp.exp2((scores - top) * scale).astype(BF16)
        both = dot(raised, jnp.concatenate([v, ones], axis=1))
        mixed = both[:, :LANES] / both[:, LANES:]
        out = mixed[:rows]
        for h in range(1, per_block):
            out = jnp.where(lane >= h * head_width, mixed[h * rows:(h + 1) * rows], out)
        outs.append(out.astype(BF16))
    return jnp.concatenate(outs, axis=1)


def kernel(
    n, x_hbm, wq1_hbm, wo1_hbm, wq2_hbm, wo2_hbm, up_hbm, down_hbm, out_hbm,
    x_v, wq1, wo1, wq2, wo2, up, down, packed, send1, recv1, send2,
    load_sem, send1_sem, recv1_sem, send2_sem, recv2_sem,
):
    _, slot, width = x_v.shape
    total = n * slot
    head_width = width // HEADS
    half = n // 2
    me = lax.axis_index("seq")
    side = me // half
    near, far = side * half, (1 - side) * half
    place = lax.rem(me, half)

    def load(i, src, dst):
        return pltpu.make_async_copy(src, dst, load_sem.at[i])

    loads = [
        load(i, src, dst) for i, (src, dst) in enumerate(
            ((x_hbm, x_v), (wq1_hbm, wq1), (wo1_hbm, wo1), (wq2_hbm, wq2), (wo2_hbm, wo2), (up_hbm, up), (down_hbm, down))
        )
    ]
    loads[0].start()
    loads[1].start()

    def far_peer(j):
        return far + lax.rem(place + j, half)

    def near_peer(j):
        return near + lax.rem(place + j, half)

    def each(first, body):
        def step(j, carry):
            body(j)
            return carry

        lax.fori_loop(first, half, step, 0, unroll=half <= 8)

    barrier = pltpu.get_barrier_semaphore()
    each(0, lambda j: pl.semaphore_signal(barrier, inc=1, device_id={"seq": far_peer(j)}, device_id_type=MESH))
    each(1, lambda j: pl.semaphore_signal(barrier, inc=1, device_id={"seq": near_peer(j)}, device_id_type=MESH))

    def copy1(peer, source):
        return pltpu.make_async_remote_copy(
            src_ref=send1.at[peer], dst_ref=recv1.at[source], send_sem=send1_sem.at[peer],
            recv_sem=recv1_sem.at[source], device_id={"seq": peer}, device_id_type=MESH,
        )

    def copy2(peer, source):
        return pltpu.make_async_remote_copy(
            src_ref=send2.at[peer], dst_ref=out_hbm.at[source], send_sem=send2_sem.at[peer],
            recv_sem=recv2_sem.at[source], device_id={"seq": peer}, device_id_type=MESH,
        )

    def every_peer(body):
        each(0, lambda j: body(far_peer(j)))
        each(1, lambda j: body(near_peer(j)))

    row_block = min(128, total)
    slots_block = row_block // slot

    def project(source, weights, i):
        rows = source[pl.ds(i * slots_block, slots_block)].astype(F32).reshape(row_block, width)
        packed[pl.ds(i * row_block, row_block), :] = dot(norm_rows(rows), weights[...]).astype(BF16)

    part = min(64, half * slot)
    part_slots = part // slot
    parts = half // part_slots

    loads[0].wait()
    loads[1].wait()
    for i in range(2, 7):
        loads[i].start()
    blocks_of(total // row_block, functools.partial(project, x_v, wq1))

    def spatial(base, i):
        first = base + i * part_slots
        heads = attend(packed, pl.multiple_of(first * slot, part), part, width, head_width, 0)
        rows = x_v[pl.ds(first, part_slots)].astype(F32).reshape(part, width)
        merged = rows + dot(heads, wo1[...])
        send1[pl.ds(first, part_slots)] = merged.reshape(part_slots, slot, width).astype(BF16)

    loads[2].wait()
    blocks_of(parts, functools.partial(spatial, far))
    pl.semaphore_wait(barrier, n - 1)
    each(0, lambda j: copy1(far_peer(j), me).start())
    blocks_of(parts, functools.partial(spatial, near))
    each(1, lambda j: copy1(near_peer(j), me).start())
    recv1[me] = send1[me]

    for i in range(3, 7):
        loads[i].wait()
    every_peer(lambda peer: copy1(me, peer).wait_recv())
    blocks_of(total // row_block, functools.partial(project, recv1, wq2))

    def temporal(base, i):
        first = base + i * part_slots
        heads = attend(packed, pl.multiple_of(first * slot, part), part, width, head_width, slot)
        rows = recv1[pl.ds(first, part_slots)].astype(F32).reshape(part, width)
        after = (rows + dot(heads, wo2[...])).astype(BF16).astype(F32)
        hidden = gelu(dot(norm_rows(after), up[...])).astype(BF16)
        done = after + dot(hidden, down[...])
        send2[pl.ds(first, part_slots)] = done.reshape(part_slots, slot, width).astype(BF16)

    blocks_of(parts, functools.partial(temporal, far))
    each(0, lambda j: copy2(far_peer(j), me).start())
    blocks_of(parts, functools.partial(temporal, near))
    each(1, lambda j: copy2(near_peer(j), me).start())
    own = pltpu.make_async_copy(send2.at[me], out_hbm.at[me], load_sem.at[0])
    own.start()
    every_peer(lambda peer: copy1(peer, me).wait_send())
    own.wait()
    every_peer(lambda peer: copy2(peer, me).wait_send())
    every_peer(lambda peer: copy2(me, peer).wait_recv())


def solution(mesh):
    n = mesh.shape["seq"]

    def local(clip_tokens, *weights):
        frames, patches, width = clip_tokens.shape
        assert frames == 1
        slot = patches // n
        blocks = (n, slot, width)
        vmem = [pltpu.VMEM(w.shape, w.dtype) for w in weights]
        out = pl.pallas_call(
            functools.partial(kernel, n),
            out_shape=jax.ShapeDtypeStruct(blocks, BF16),
            in_specs=[pl.BlockSpec(memory_space=pl.ANY)] * 7,
            out_specs=pl.BlockSpec(memory_space=pl.ANY),
            scratch_shapes=[
                pltpu.VMEM(blocks, BF16),
                *vmem,
                pltpu.VMEM((patches, 3 * width), BF16),
                pltpu.VMEM(blocks, BF16),
                pltpu.VMEM(blocks, BF16),
                pltpu.VMEM(blocks, BF16),
                pltpu.SemaphoreType.DMA((7,)),
                pltpu.SemaphoreType.DMA((n,)),
                pltpu.SemaphoreType.DMA((n,)),
                pltpu.SemaphoreType.DMA((n,)),
                pltpu.SemaphoreType.DMA((n,)),
            ],
            compiler_params=pltpu.CompilerParams(collective_id=0, has_side_effects=True),
            name="layer",
        )(clip_tokens.reshape(blocks), *weights)
        return out.reshape(frames, patches, width)

    in_specs = (P(("groups", "seq"), None, None), P(), P(), P(), P(), P(), P())
    out_specs = P(("groups", "seq"), None, None)
    return jax.shard_map(local, mesh=mesh, in_specs=in_specs, out_specs=out_specs, check_vma=False)
```

```python
import functools
import math

import jax
import jax.numpy as jnp
from jax import lax
from jax.experimental import pallas as pl
from jax.experimental.pallas import tpu as pltpu
from jax.sharding import PartitionSpec as P

HEADS = 8
LANES = 128
VMEM_BYTES = 67043328
MESH = pl.DeviceIdType.MESH
F32 = jnp.float32
BF16 = jnp.bfloat16


def norm_rows(values):
    center = values - jnp.mean(values, axis=-1, keepdims=True)
    spread = jnp.mean(center * center, axis=-1, keepdims=True)
    return (center * lax.rsqrt(spread + 1e-05)).astype(BF16)


def gelu(u):
    return 0.5 * u * (1.0 + jnp.tanh(math.sqrt(2.0 / math.pi) * (u + 0.044715 * (u * u * u))))


def dot(a, b):
    return jnp.dot(a, b, preferred_element_type=F32)


def blocks_of(count, body):
    if count <= 2:
        for i in range(count):
            body(i)
    else:
        def step(i, carry):
            body(i)
            return carry

        lax.fori_loop(0, count, step, 0)


def attend(packed, first_row, rows, width, head_width, same_slot):
    total = packed.shape[0]
    per_block = LANES // head_width
    lane = lax.broadcasted_iota(jnp.int32, (rows, LANES), 1)
    ones = jnp.ones((total, LANES), BF16)
    scale = head_width ** (-0.5) * math.log2(math.e)
    if same_slot:
        query_at = lax.broadcasted_iota(jnp.int32, (per_block * rows, total), 0)
        key_at = lax.broadcasted_iota(jnp.int32, (per_block * rows, total), 1)
        allowed = lax.rem(query_at, same_slot) == lax.rem(key_at, same_slot)
    outs = []
    for block in range(width // LANES):
        q = packed[pl.ds(first_row, rows), pl.ds(block * LANES, LANES)]
        k = packed[:, pl.ds(width + block * LANES, LANES)]
        v = packed[:, pl.ds(2 * width + block * LANES, LANES)]
        split = [
            jnp.where((lane >= h * head_width) & (lane < (h + 1) * head_width), q, jnp.zeros_like(q))
            for h in range(per_block)
        ]
        scores = lax.dot_general(
            jnp.concatenate(split, axis=0), k, (((1,), (1,)), ((), ())), preferred_element_type=F32
        )
        if same_slot:
            scores = jnp.where(allowed, scores, -1e30)
        top = jnp.max(scores, axis=-1, keepdims=True)
        raised = jnp.exp2((scores - top) * scale).astype(BF16)
        both = dot(raised, jnp.concatenate([v, ones], axis=1))
        mixed = both[:, :LANES] / both[:, LANES:]
        out = mixed[:rows]
        for h in range(1, per_block):
            out = jnp.where(lane >= h * head_width, mixed[h * rows:(h + 1) * rows], out)
        outs.append(out.astype(BF16))
    return jnp.concatenate(outs, axis=1)


def kernel(
    n, x_hbm, wq1_hbm, wo1_hbm, wq2_hbm, wo2_hbm, up_hbm, down_hbm, out_v,
    x_v, wq1, wo1, wq2, wo2, up, down, packed, send1, recv1, send2,
    load_sem, send1_sem, recv1_sem, send2_sem, recv2_sem,
):
    _, slot, width = x_v.shape
    total = n * slot
    head_width = width // HEADS
    half = n // 2
    me = lax.axis_index("seq")
    side = me // half
    near, far = side * half, (1 - side) * half
    place = lax.rem(me, half)

    def load(i, src, dst):
        return pltpu.make_async_copy(src, dst, load_sem.at[i])

    loads = [
        load(i, src, dst) for i, (src, dst) in enumerate(
            ((x_hbm, x_v), (wq1_hbm, wq1), (wo1_hbm, wo1), (wq2_hbm, wq2), (wo2_hbm, wo2), (up_hbm, up), (down_hbm, down))
        )
    ]
    loads[0].start()
    loads[1].start()

    def far_peer(j):
        return far + lax.rem(place + j, half)

    def near_peer(j):
        return near + lax.rem(place + j, half)

    def each(first, body):
        def step(j, carry):
            body(j)
            return carry

        lax.fori_loop(first, half, step, 0, unroll=half <= 8)

    barrier = pltpu.get_barrier_semaphore()
    each(0, lambda j: pl.semaphore_signal(barrier, inc=1, device_id={"seq": far_peer(j)}, device_id_type=MESH))
    each(1, lambda j: pl.semaphore_signal(barrier, inc=1, device_id={"seq": near_peer(j)}, device_id_type=MESH))

    def copy1(peer, source):
        return pltpu.make_async_remote_copy(
            src_ref=send1.at[peer], dst_ref=recv1.at[source], send_sem=send1_sem.at[peer],
            recv_sem=recv1_sem.at[source], device_id={"seq": peer}, device_id_type=MESH,
        )

    def copy2(peer, source):
        return pltpu.make_async_remote_copy(
            src_ref=send2.at[peer], dst_ref=out_v.at[source], send_sem=send2_sem.at[peer],
            recv_sem=recv2_sem.at[source], device_id={"seq": peer}, device_id_type=MESH,
        )

    def every_peer(body):
        each(0, lambda j: body(far_peer(j)))
        each(1, lambda j: body(near_peer(j)))

    row_block = min(128, total)
    slots_block = row_block // slot

    def project(source, weights, i):
        rows = source[pl.ds(i * slots_block, slots_block)].astype(F32).reshape(row_block, width)
        packed[pl.ds(i * row_block, row_block), :] = dot(norm_rows(rows), weights[...]).astype(BF16)

    part = min(64, half * slot)
    part_slots = part // slot
    parts = half // part_slots

    loads[0].wait()
    loads[1].wait()
    for i in range(2, 7):
        loads[i].start()
    blocks_of(total // row_block, functools.partial(project, x_v, wq1))

    def spatial(base, i):
        first = base + i * part_slots
        heads = attend(packed, pl.multiple_of(first * slot, part), part, width, head_width, 0)
        rows = x_v[pl.ds(first, part_slots)].astype(F32).reshape(part, width)
        merged = rows + dot(heads, wo1[...])
        send1[pl.ds(first, part_slots)] = merged.reshape(part_slots, slot, width).astype(BF16)

    loads[2].wait()
    blocks_of(parts, functools.partial(spatial, far))
    pl.semaphore_wait(barrier, n - 1)
    each(0, lambda j: copy1(far_peer(j), me).start())
    blocks_of(parts, functools.partial(spatial, near))
    each(1, lambda j: copy1(near_peer(j), me).start())
    recv1[me] = send1[me]

    for i in range(3, 7):
        loads[i].wait()
    every_peer(lambda peer: copy1(me, peer).wait_recv())
    blocks_of(total // row_block, functools.partial(project, recv1, wq2))

    def temporal(base, i):
        first = base + i * part_slots
        heads = attend(packed, pl.multiple_of(first * slot, part), part, width, head_width, slot)
        rows = recv1[pl.ds(first, part_slots)].astype(F32).reshape(part, width)
        after = (rows + dot(heads, wo2[...])).astype(BF16).astype(F32)
        hidden = gelu(dot(norm_rows(after), up[...])).astype(BF16)
        done = after + dot(hidden, down[...])
        send2[pl.ds(first, part_slots)] = done.reshape(part_slots, slot, width).astype(BF16)

    blocks_of(parts, functools.partial(temporal, far))
    each(0, lambda j: copy2(far_peer(j), me).start())
    blocks_of(parts, functools.partial(temporal, near))
    each(1, lambda j: copy2(near_peer(j), me).start())
    out_v[me] = send2[me]
    every_peer(lambda peer: copy1(peer, me).wait_send())
    every_peer(lambda peer: copy2(peer, me).wait_send())
    every_peer(lambda peer: copy2(me, peer).wait_recv())


def store(rows_v, out_hbm, sem):
    copy = pltpu.make_async_copy(rows_v, out_hbm, sem)
    copy.start()
    copy.wait()


def solution(mesh):
    n = mesh.shape["seq"]

    def local(clip_tokens, *weights):
        frames, patches, width = clip_tokens.shape
        assert frames == 1
        slot = patches // n
        blocks = (n, slot, width)
        vmem = [pltpu.VMEM(w.shape, w.dtype) for w in weights]
        out = pl.pallas_call(
            functools.partial(kernel, n),
            out_shape=pltpu.VMEM(blocks, BF16),
            in_specs=[pl.BlockSpec(memory_space=pltpu.HBM)] * 7,
            out_specs=pl.BlockSpec(memory_space=pltpu.VMEM),
            scratch_shapes=[
                pltpu.VMEM(blocks, BF16),
                *vmem,
                pltpu.VMEM((patches, 3 * width), BF16),
                pltpu.VMEM(blocks, BF16),
                pltpu.VMEM(blocks, BF16),
                pltpu.VMEM(blocks, BF16),
                pltpu.SemaphoreType.DMA((7,)),
                pltpu.SemaphoreType.DMA((n,)),
                pltpu.SemaphoreType.DMA((n,)),
                pltpu.SemaphoreType.DMA((n,)),
                pltpu.SemaphoreType.DMA((n,)),
            ],
            compiler_params=pltpu.CompilerParams(collective_id=0, has_side_effects=True, vmem_limit_bytes=VMEM_BYTES - math.prod(blocks) * 2 - 65536),
            name="layer",
        )(clip_tokens.reshape(blocks), *weights)
        return out.reshape(frames, patches, width)

    in_specs = (P(("groups", "seq"), None, None), P(), P(), P(), P(), P(), P())
    out_specs = P(("groups", "seq"), None, None)
    return jax.shard_map(local, mesh=mesh, in_specs=in_specs, out_specs=out_specs, check_vma=False)
```

```python
import functools
import math

import jax
import jax.numpy as jnp
from jax import lax
from jax.experimental import pallas as pl
from jax.experimental.pallas import tpu as pltpu
from jax.sharding import PartitionSpec as P

HEADS = 8
LANES = 128
VMEM_BYTES = 67043328
MESH = pl.DeviceIdType.MESH
F32 = jnp.float32
BF16 = jnp.bfloat16


def norm_rows(values):
    center = values - jnp.mean(values, axis=-1, keepdims=True)
    spread = jnp.mean(center * center, axis=-1, keepdims=True)
    return (center * lax.rsqrt(spread + 1e-05)).astype(BF16)


def gelu(u):
    return 0.5 * u * (1.0 + jnp.tanh(math.sqrt(2.0 / math.pi) * (u + 0.044715 * (u * u * u))))


def dot(a, b):
    return jnp.dot(a, b, preferred_element_type=F32)


def blocks_of(count, body):
    if count <= 2:
        for i in range(count):
            body(i)
    else:
        def step(i, carry):
            body(i)
            return carry

        lax.fori_loop(0, count, step, 0)


def attend(packed, first_row, rows, width, head_width, same_slot):
    total = packed.shape[0]
    per_block = LANES // head_width
    lane = lax.broadcasted_iota(jnp.int32, (rows, LANES), 1)
    ones = jnp.ones((total, LANES), BF16)
    scale = head_width ** (-0.5) * math.log2(math.e)
    if same_slot:
        query_at = lax.broadcasted_iota(jnp.int32, (per_block * rows, total), 0)
        key_at = lax.broadcasted_iota(jnp.int32, (per_block * rows, total), 1)
        allowed = lax.rem(query_at, same_slot) == lax.rem(key_at, same_slot)
    outs = []
    for block in range(width // LANES):
        q = packed[pl.ds(first_row, rows), pl.ds(block * LANES, LANES)]
        k = packed[:, pl.ds(width + block * LANES, LANES)]
        v = packed[:, pl.ds(2 * width + block * LANES, LANES)]
        split = [
            jnp.where((lane >= h * head_width) & (lane < (h + 1) * head_width), q, jnp.zeros_like(q))
            for h in range(per_block)
        ]
        scores = lax.dot_general(
            jnp.concatenate(split, axis=0), k, (((1,), (1,)), ((), ())), preferred_element_type=F32
        )
        if same_slot:
            scores = jnp.where(allowed, scores, -1e30)
        top = jnp.max(scores, axis=-1, keepdims=True)
        raised = jnp.exp2((scores - top) * scale).astype(BF16)
        both = dot(raised, jnp.concatenate([v, ones], axis=1))
        mixed = both[:, :LANES] / both[:, LANES:]
        out = mixed[:rows]
        for h in range(1, per_block):
            out = jnp.where(lane >= h * head_width, mixed[h * rows:(h + 1) * rows], out)
        outs.append(out.astype(BF16))
    return jnp.concatenate(outs, axis=1)


def kernel(
    n, x_hbm, wq1_hbm, wo1_hbm, wq2_hbm, wo2_hbm, up_hbm, down_hbm, out_v,
    x_v, wq1, wo1, wq2, wo2, up, down, packed, normed, send1, recv1, send2,
    load_sem, send1_sem, recv1_sem, send2_sem, recv2_sem,
):
    _, slot, width = x_v.shape
    total = n * slot
    head_width = width // HEADS
    half = n // 2
    me = lax.axis_index("seq")
    side = me // half
    near, far = side * half, (1 - side) * half
    place = lax.rem(me, half)

    def load(i, src, dst):
        return pltpu.make_async_copy(src, dst, load_sem.at[i])

    loads = [
        load(i, src, dst) for i, (src, dst) in enumerate(
            ((x_hbm, x_v), (wq1_hbm, wq1), (wo1_hbm, wo1), (wq2_hbm, wq2), (wo2_hbm, wo2), (up_hbm, up), (down_hbm, down))
        )
    ]
    bands = [pl.ds(b * width, width) for b in range(3)]
    band_loads = [load(i, wq1_hbm.at[:, band], wq1.at[:, band]) for i, band in zip((1, 7, 8), bands)]
    loads[0].start()
    for band_load in band_loads:
        band_load.start()

    def far_peer(j):
        return far + lax.rem(place + j, half)

    def near_peer(j):
        return near + lax.rem(place + j, half)

    def each(first, body):
        def step(j, carry):
            body(j)
            return carry

        lax.fori_loop(first, half, step, 0, unroll=half <= 8)

    barrier = pltpu.get_barrier_semaphore()
    each(0, lambda j: pl.semaphore_signal(barrier, inc=1, device_id={"seq": far_peer(j)}, device_id_type=MESH))
    each(1, lambda j: pl.semaphore_signal(barrier, inc=1, device_id={"seq": near_peer(j)}, device_id_type=MESH))

    def copy1(peer, source):
        return pltpu.make_async_remote_copy(
            src_ref=send1.at[peer], dst_ref=recv1.at[source], send_sem=send1_sem.at[peer],
            recv_sem=recv1_sem.at[source], device_id={"seq": peer}, device_id_type=MESH,
        )

    def copy2(peer, source):
        return pltpu.make_async_remote_copy(
            src_ref=send2.at[peer], dst_ref=out_v.at[source], send_sem=send2_sem.at[peer],
            recv_sem=recv2_sem.at[source], device_id={"seq": peer}, device_id_type=MESH,
        )

    def every_peer(body):
        each(0, lambda j: body(far_peer(j)))
        each(1, lambda j: body(near_peer(j)))

    row_block = min(128, total)
    slots_block = row_block // slot

    def project(source, weights, i):
        rows = source[pl.ds(i * slots_block, slots_block)].astype(F32).reshape(row_block, width)
        packed[pl.ds(i * row_block, row_block), :] = dot(norm_rows(rows), weights[...]).astype(BF16)

    part = min(64, half * slot)
    part_slots = part // slot
    parts = half // part_slots

    loads[0].wait()
    for i in range(2, 7):
        loads[i].start()

    def normalise(i):
        rows = x_v[pl.ds(i * slots_block, slots_block)].astype(F32).reshape(row_block, width)
        normed[pl.ds(i * row_block, row_block), :] = norm_rows(rows)

    def project_band(band, i):
        at = pl.ds(i * row_block, row_block)
        packed[at, band] = dot(normed[at, :], wq1[:, band]).astype(BF16)

    blocks_of(total // row_block, normalise)
    for band, band_load in zip(bands, band_loads):
        band_load.wait()
        blocks_of(total // row_block, functools.partial(project_band, band))

    def spatial(base, i):
        first = base + i * part_slots
        heads = attend(packed, pl.multiple_of(first * slot, part), part, width, head_width, 0)
        rows = x_v[pl.ds(first, part_slots)].astype(F32).reshape(part, width)
        merged = rows + dot(heads, wo1[...])
        send1[pl.ds(first, part_slots)] = merged.reshape(part_slots, slot, width).astype(BF16)

    loads[2].wait()
    blocks_of(parts, functools.partial(spatial, far))
    pl.semaphore_wait(barrier, n - 1)
    each(0, lambda j: copy1(far_peer(j), me).start())
    blocks_of(parts, functools.partial(spatial, near))
    each(1, lambda j: copy1(near_peer(j), me).start())
    recv1[me] = send1[me]

    for i in range(3, 7):
        loads[i].wait()
    every_peer(lambda peer: copy1(me, peer).wait_recv())
    blocks_of(total // row_block, functools.partial(project, recv1, wq2))

    def temporal(base, i):
        first = base + i * part_slots
        heads = attend(packed, pl.multiple_of(first * slot, part), part, width, head_width, slot)
        rows = recv1[pl.ds(first, part_slots)].astype(F32).reshape(part, width)
        after = (rows + dot(heads, wo2[...])).astype(BF16).astype(F32)
        hidden = gelu(dot(norm_rows(after), up[...])).astype(BF16)
        done = after + dot(hidden, down[...])
        send2[pl.ds(first, part_slots)] = done.reshape(part_slots, slot, width).astype(BF16)

    blocks_of(parts, functools.partial(temporal, far))
    each(0, lambda j: copy2(far_peer(j), me).start())
    blocks_of(parts, functools.partial(temporal, near))
    each(1, lambda j: copy2(near_peer(j), me).start())
    out_v[me] = send2[me]
    every_peer(lambda peer: copy1(peer, me).wait_send())
    every_peer(lambda peer: copy2(peer, me).wait_send())
    every_peer(lambda peer: copy2(me, peer).wait_recv())


def store(rows_v, out_hbm, sem):
    copy = pltpu.make_async_copy(rows_v, out_hbm, sem)
    copy.start()
    copy.wait()


def solution(mesh):
    n = mesh.shape["seq"]

    def local(clip_tokens, *weights):
        frames, patches, width = clip_tokens.shape
        assert frames == 1
        slot = patches // n
        blocks = (n, slot, width)
        vmem = [pltpu.VMEM(w.shape, w.dtype) for w in weights]
        out = pl.pallas_call(
            functools.partial(kernel, n),
            out_shape=pltpu.VMEM(blocks, BF16),
            in_specs=[pl.BlockSpec(memory_space=pltpu.HBM)] * 7,
            out_specs=pl.BlockSpec(memory_space=pltpu.VMEM),
            scratch_shapes=[
                pltpu.VMEM(blocks, BF16),
                *vmem,
                pltpu.VMEM((patches, 3 * width), BF16),
                pltpu.VMEM((patches, width), BF16),
                pltpu.VMEM(blocks, BF16),
                pltpu.VMEM(blocks, BF16),
                pltpu.VMEM(blocks, BF16),
                pltpu.SemaphoreType.DMA((9,)),
                pltpu.SemaphoreType.DMA((n,)),
                pltpu.SemaphoreType.DMA((n,)),
                pltpu.SemaphoreType.DMA((n,)),
                pltpu.SemaphoreType.DMA((n,)),
            ],
            compiler_params=pltpu.CompilerParams(collective_id=0, has_side_effects=True, vmem_limit_bytes=VMEM_BYTES - math.prod(blocks) * 2 - 65536),
            name="layer",
        )(clip_tokens.reshape(blocks), *weights)
        return out.reshape(frames, patches, width)

    in_specs = (P(("groups", "seq"), None, None), P(), P(), P(), P(), P(), P())
    out_specs = P(("groups", "seq"), None, None)
    return jax.shard_map(local, mesh=mesh, in_specs=in_specs, out_specs=out_specs, check_vma=False)
```
